32 devices in a mesh: groups: 2 (over y), blk: 4 (over z), team: 2 (over x), head: 2 (over core).
Axes of the slice: x: 2, y: 2, z: 4, core: 2. Of those that a mesh axis runs over, the one named last changes fastest.
Arguments:
- queries: bfloat16 [768, 2560], P(('groups', 'blk', 'team'), 'head'), parts along dimension 0, may hold values from -8 to 8
- key_rows: bfloat16 [768, 2560], P(('groups', 'blk', 'team'), 'head'), parts along dimension 0, may hold values from -8 to 8
- value_rows: bfloat16 [768, 2560], P(('groups', 'blk', 'team'), 'head'), parts along dimension 0, may hold values from -6 to 6
Outputs:
- attended: bfloat16 [768, 2560], P(('groups', 'blk', 'team'), 'head'), parts along dimension 0
The draws below stay inside these ranges and needn't reach their ends.
There are 2 independent parts, one for each index of `groups`. The reference program is written for one: setup_inputs(seed, part) draws one part's arguments, and reference() takes and returns one part's arrays. A program takes and returns all parts, laid end to end along the dimension named above; each array names one. Nothing has to cross between parts.
All inputs are finite; a program needn't handle non-finite values.
Results may differ from the reference program's by a relative error of at most 0.009.
Values may be sent and summed in bfloat16 or wider, within the bound.
No kernel may reach another device: no remote copies, remote signals or barrier semaphores. Data moves between devices by JAX's collectives and lax.ppermute only.
A program may use at most 64 MiB of HBM per device.

```python
import math
import jax
import jax.numpy as jnp
from jax import lax

HD = 128
H = 20
SEQ = 384


def rough_rows(base_key, salt_value):
    noise_key = jax.random.fold_in(base_key, salt_value)
    return jax.random.normal(noise_key, (SEQ, H * HD), jnp.float32)


def draw_queries(key, part):
    entries = rough_rows(key, 1)
    return jnp.clip(entries, -8.0, 8.0).astype(jnp.bfloat16)


def draw_key_rows(key, part):
    entries = rough_rows(key, 2)
    return jnp.clip(entries, -8.0, 8.0).astype(jnp.bfloat16)


def block_scale(own_key, dims, pieces, low, high):
    loudness, own = 1.0, jax.random.fold_in(own_key, 6)
    for dim, parts in pieces:
        draws = jnp.exp(jax.random.uniform(jax.random.fold_in(own, dim), (parts,), jnp.float32, low / len(pieces), high / len(pieces)))
        loudness = loudness * jnp.repeat(draws, dims[dim] // parts).reshape([-1 if axis == dim else 1 for axis in range(len(dims))])
    return loudness


def scatter_about(rng, extent, scale, bound, shards=(), dtype=jnp.bfloat16):
    result = scale * jax.random.normal(rng, extent, jnp.float32)
    if shards:
        result = result * block_scale(rng, extent, shards, -0.22, 0.18)
    return jnp.clip(result, -bound, bound).astype(dtype)


def setup_inputs(seed: int = 0, part: int = 0) -> dict:
    seeds = jax.random.split(jax.random.key(seed), 4)
    part_splits = jax.random.split(jax.random.fold_in(seeds[3], part), 4)
    return {
        "queries": draw_queries(jax.random.fold_in(jax.random.fold_in(seeds[3], part), 71), part),
        "key_rows": draw_key_rows(jax.random.fold_in(jax.random.fold_in(seeds[3], part), 71), part),
        "value_rows": scatter_about(part_splits[2], (SEQ, H * HD), 1.0, 6.0, ((0, 8), (1, 2))),
    }


def one_head(operands):
    query_head, key_head, value_head = operands
    scores = jnp.dot(query_head, key_head.T, preferred_element_type=jnp.float32) * (1.0 / math.sqrt(HD))
    row_top = lax.optimization_barrier(jnp.max(scores, axis=1, keepdims=True))
    weights = jnp.exp(scores - row_top)
    row_total = lax.optimization_barrier(jnp.sum(weights, axis=1, keepdims=True))
    mixed_head = jnp.dot(weights.astype(jnp.bfloat16), value_head, preferred_element_type=jnp.float32)
    return (mixed_head / row_total).astype(jnp.bfloat16)

def by_head(matrix):
    return matrix.reshape(SEQ, H, HD).transpose(1, 0, 2)

def reference(queries, key_rows, value_rows):
    attended = lax.map(one_head, (by_head(queries), by_head(key_rows), by_head(value_rows)))
    return attended.transpose(1, 0, 2).reshape(SEQ, H * HD)
```

```python
from functools import partial
import math

import jax
import jax.numpy as jnp
from jax import lax
from jax.experimental import pallas as pl
from jax.experimental.pallas import tpu as pltpu
from jax.sharding import PartitionSpec as P

HD = 128
T_DEV = 48


def attend_block(running, key_block, value_block, query_rows, score_scale):
    row_top, row_total, weighted = running
    scores = (
        jnp.einsum("qhd,khd->qhk", query_rows, key_block, preferred_element_type=jnp.float32)
        * score_scale
    )
    new_top = jnp.maximum(row_top, jnp.max(scores, axis=2))
    shrink = jnp.exp(row_top - new_top)
    weights = jnp.exp(scores - new_top[:, :, None])
    row_total = row_total * shrink + jnp.sum(weights, axis=2)
    weighted = weighted * shrink[:, :, None] + jnp.einsum(
        "qhk,khd->qhd",
        weights.astype(jnp.bfloat16),
        value_block,
        preferred_element_type=jnp.float32,
    )
    return (new_top, row_total, weighted)


def fold_piece(running, shard_piece, query_rows, score_scale):
    key_piece, value_piece = shard_piece
    piece_rows = key_piece.shape[0]
    block_rows = T_DEV
    local_heads = query_rows.shape[1]
    key_blocks = key_piece.reshape(piece_rows // block_rows, block_rows, local_heads, HD)
    value_blocks = value_piece.reshape(piece_rows // block_rows, block_rows, local_heads, HD)

    def one_block(current, block_pair):
        return (attend_block(current, block_pair[0], block_pair[1], query_rows, score_scale), None)

    running, unused = lax.scan(one_block, running, (key_blocks, value_blocks))
    return running


def gathered(queries, key_rows, value_rows):
    own_rows = queries.shape[0]
    local_heads = queries.shape[1] // HD
    score_scale = 1.0 / math.sqrt(HD)
    team_queries = lax.all_gather(queries, "team", axis=0, tiled=True)
    team_count = team_queries.shape[0]
    query_heads = team_queries.reshape(team_count, local_heads, HD)
    folder = partial(fold_piece, query_rows=query_heads, score_scale=score_scale)
    row_top, row_total, weighted = folder(
        (
            jnp.full((team_count, local_heads), -1e30, jnp.float32),
            jnp.zeros((team_count, local_heads), jnp.float32),
            jnp.zeros((team_count, local_heads, HD), jnp.float32),
        ),
        (
            lax.all_gather(key_rows, "blk", axis=0, tiled=True),
            lax.all_gather(value_rows, "blk", axis=0, tiled=True),
        ),
    )
    swapped, member_tops, totals = (
        lax.all_to_all(
            weighted.reshape(team_count, local_heads * HD),
            "team",
            split_axis=0,
            concat_axis=0,
            tiled=True,
        ),
        lax.all_to_all(row_top, "team", split_axis=0, concat_axis=0, tiled=True),
        lax.all_to_all(row_total, "team", split_axis=0, concat_axis=0, tiled=True),
    )
    members = lax.axis_size("team")
    member_tops = member_tops.reshape(members, own_rows, local_heads)
    common_top = jnp.max(member_tops, axis=0)
    factor = jnp.exp(member_tops - common_top[None])
    row_sum = jnp.sum(factor * totals.reshape(members, own_rows, local_heads), axis=0)
    summed = jnp.sum(
        factor[:, :, :, None] * swapped.reshape(members, own_rows, local_heads, HD), axis=0
    )
    mixed_rows = summed / row_sum[:, :, None]
    return mixed_rows.reshape(own_rows, local_heads * HD).astype(jnp.bfloat16)


def group_start(plane, planes, heads, group):
    return plane * (heads - group) // (planes - 1) if planes > 1 else plane * 0


def pack_kernel(planes, heads, group, q_ref, k_ref, v_ref, *refs):
    outs, sems = refs[:-1], refs[-1]
    own = lax.axis_index("blk")
    rows = q_ref.shape[0]
    copies = []
    for r in list(range(1, planes)) + [0]:
        plane = lax.rem(own + r, planes)
        first = pl.multiple_of(group_start(plane, planes, heads, group) * HD, HD)
        columns = pl.ds(first, group * HD)
        kv_out, q_out = outs[2 * r], outs[2 * r + 1]
        for source, target in (
            (k_ref, kv_out.at[pl.ds(0, rows)]),
            (v_ref, kv_out.at[pl.ds(rows, rows)]),
            (q_ref, q_out),
        ):
            copy = pltpu.make_async_copy(source.at[:, columns], target, sems.at[len(copies)])
            copy.start()
            copies.append(copy)
    for copy in copies:
        copy.wait()


def attend_kernel(planes, members, group, *refs):
    pieces = refs[: planes * members]
    q_refs = refs[planes * members : planes * members + planes]
    o_refs = refs[planes * members + planes :]
    rows = q_refs[0].shape[0]
    scale = 1.0 / math.sqrt(HD)
    for h in range(group):
        columns = slice(h * HD, (h + 1) * HD)
        q = jnp.concatenate([ref[:, columns] for ref in q_refs], axis=0)
        k = jnp.concatenate([ref[:rows, columns] for ref in pieces], axis=0)
        v = jnp.concatenate([ref[rows:, columns] for ref in pieces], axis=0)
        scores = lax.dot_general(q, k, (((1,), (1,)), ((), ())), preferred_element_type=jnp.float32) * scale
        weights = jnp.exp(scores - jnp.max(scores, axis=1, keepdims=True))
        total = jnp.sum(weights, axis=1, keepdims=True)
        mixed = jnp.dot(weights.astype(jnp.bfloat16), v, preferred_element_type=jnp.float32)
        out = (mixed / total).astype(jnp.bfloat16)
        for i, ref in enumerate(o_refs):
            ref[:, columns] = out[i * rows : (i + 1) * rows]


def unpack_kernel(planes, heads, group, *refs):
    pieces, out_ref = refs[:-1], refs[-1]
    own = lax.axis_index("blk")
    for r, piece in enumerate(pieces):
        plane = lax.rem(own + r, planes)
        first = pl.multiple_of(group_start(plane, planes, heads, group) * HD, HD)
        out_ref[:, pl.ds(first, group * HD)] = piece[...]


def exchanged(queries, key_rows, value_rows):
    rows = queries.shape[0]
    heads = queries.shape[1] // HD
    planes, members = lax.axis_size("blk"), lax.axis_size("team")
    group = -(-heads // planes)
    width = group * HD
    limit = 16 * 2**20
    vmem = pl.BlockSpec(memory_space=pltpu.VMEM)
    hbm = pl.BlockSpec(memory_space=pltpu.HBM)
    kv_shape = jax.ShapeDtypeStruct((2 * rows, width), queries.dtype)
    q_shape = jax.ShapeDtypeStruct((rows, width), queries.dtype)

    packed = pl.pallas_call(
        partial(pack_kernel, planes, heads, group),
        out_shape=[kv_shape, q_shape] * planes,
        in_specs=[hbm] * 3,
        out_specs=[vmem] * (2 * planes),
        scratch_shapes=[pltpu.SemaphoreType.DMA((3 * planes,))],
        compiler_params=pltpu.CompilerParams(vmem_limit_bytes=limit),
        name="pack",
    )(*(pltpu.with_memory_space_constraint(a, pltpu.HBM) for a in (queries, key_rows, value_rows)))

    def turn(array, r):
        return lax.ppermute(array, "blk", [(i, (i + r) % planes) for i in range(planes)])

    kv = [packed[0]] + [turn(packed[2 * r], r) for r in range(1, planes)]
    q = [packed[1]] + [turn(packed[2 * r + 1], r) for r in range(1, planes)]
    pieces = list(kv)
    for m in range(1, members):
        pieces += [
            lax.ppermute(piece, "team", [(i, (i + m) % members) for i in range(members)])
            for piece in kv
        ]
    attended = pl.pallas_call(
        partial(attend_kernel, planes, members, group),
        out_shape=[q_shape] * planes,
        in_specs=[vmem] * (planes * members + planes),
        out_specs=[vmem] * planes,
        compiler_params=pltpu.CompilerParams(vmem_limit_bytes=limit),
        name="attend",
    )(*pieces, *q)
    back = [attended[0]] + [turn(attended[r], planes - r) for r in range(1, planes)]
    return pl.pallas_call(
        partial(unpack_kernel, planes, heads, group),
        out_shape=jax.ShapeDtypeStruct(queries.shape, queries.dtype),
        in_specs=[vmem] * planes,
        out_specs=vmem,
        compiler_params=pltpu.CompilerParams(vmem_limit_bytes=limit),
        name="unpack",
    )(*back)


def solution(mesh):
    spec = P(("groups", "blk", "team"), "head")

    def local(queries, key_rows, value_rows):
        heads = queries.shape[1] // HD
        plan = exchanged if mesh.shape["blk"] <= heads else gathered
        return plan(queries, key_rows, value_rows)

    return jax.shard_map(
        local, mesh=mesh, in_specs=(spec,) * 3, out_specs=spec, check_vma=False
    )
```

```python
from functools import partial
import math

import jax
import jax.numpy as jnp
from jax import lax
from jax.experimental import pallas as pl
from jax.experimental.pallas import tpu as pltpu
from jax.sharding import PartitionSpec as P

HD = 128
T_DEV = 48


def attend_block(running, key_block, value_block, query_rows, score_scale):
    row_top, row_total, weighted = running
    scores = (
        jnp.einsum("qhd,khd->qhk", query_rows, key_block, preferred_element_type=jnp.float32)
        * score_scale
    )
    new_top = jnp.maximum(row_top, jnp.max(scores, axis=2))
    shrink = jnp.exp(row_top - new_top)
    weights = jnp.exp(scores - new_top[:, :, None])
    row_total = row_total * shrink + jnp.sum(weights, axis=2)
    weighted = weighted * shrink[:, :, None] + jnp.einsum(
        "qhk,khd->qhd",
        weights.astype(jnp.bfloat16),
        value_block,
        preferred_element_type=jnp.float32,
    )
    return (new_top, row_total, weighted)


def fold_piece(running, shard_piece, query_rows, score_scale):
    key_piece, value_piece = shard_piece
    piece_rows = key_piece.shape[0]
    block_rows = T_DEV
    local_heads = query_rows.shape[1]
    key_blocks = key_piece.reshape(piece_rows // block_rows, block_rows, local_heads, HD)
    value_blocks = value_piece.reshape(piece_rows // block_rows, block_rows, local_heads, HD)

    def one_block(current, block_pair):
        return (attend_block(current, block_pair[0], block_pair[1], query_rows, score_scale), None)

    running, unused = lax.scan(one_block, running, (key_blocks, value_blocks))
    return running


def gathered(queries, key_rows, value_rows):
    own_rows = queries.shape[0]
    local_heads = queries.shape[1] // HD
    score_scale = 1.0 / math.sqrt(HD)
    team_queries = lax.all_gather(queries, "team", axis=0, tiled=True)
    team_count = team_queries.shape[0]
    query_heads = team_queries.reshape(team_count, local_heads, HD)
    folder = partial(fold_piece, query_rows=query_heads, score_scale=score_scale)
    row_top, row_total, weighted = folder(
        (
            jnp.full((team_count, local_heads), -1e30, jnp.float32),
            jnp.zeros((team_count, local_heads), jnp.float32),
            jnp.zeros((team_count, local_heads, HD), jnp.float32),
        ),
        (
            lax.all_gather(key_rows, "blk", axis=0, tiled=True),
            lax.all_gather(value_rows, "blk", axis=0, tiled=True),
        ),
    )
    swapped, member_tops, totals = (
        lax.all_to_all(
            weighted.reshape(team_count, local_heads * HD),
            "team",
            split_axis=0,
            concat_axis=0,
            tiled=True,
        ),
        lax.all_to_all(row_top, "team", split_axis=0, concat_axis=0, tiled=True),
        lax.all_to_all(row_total, "team", split_axis=0, concat_axis=0, tiled=True),
    )
    members = lax.axis_size("team")
    member_tops = member_tops.reshape(members, own_rows, local_heads)
    common_top = jnp.max(member_tops, axis=0)
    factor = jnp.exp(member_tops - common_top[None])
    row_sum = jnp.sum(factor * totals.reshape(members, own_rows, local_heads), axis=0)
    summed = jnp.sum(
        factor[:, :, :, None] * swapped.reshape(members, own_rows, local_heads, HD), axis=0
    )
    mixed_rows = summed / row_sum[:, :, None]
    return mixed_rows.reshape(own_rows, local_heads * HD).astype(jnp.bfloat16)


PARTS = 5
GAP = 128 // 8


def vmem_spec():
    return pl.BlockSpec(memory_space=pltpu.VMEM)


def hbm_array(array):
    return pltpu.with_memory_space_constraint(array, pltpu.HBM)


def params():
    return pltpu.CompilerParams(vmem_limit_bytes=16 * 2**20)


def terms(values, count):
    out = []
    for _ in range(count):
        term = values.astype(jnp.bfloat16).astype(jnp.float32)
        out.append(term)
        values = values - term
    return out


def pack_kernel(width, q_ref, k_ref, v_ref, kv_own, kv_other, kvq_other, q_own, q_other, sems):
    rows = q_ref.shape[0]
    half = lax.rem(lax.axis_index("blk"), 2)
    own = pl.ds(pl.multiple_of(half * width, HD), width)
    other = pl.ds(pl.multiple_of((1 - half) * width, HD), width)
    first, second, third = (pl.ds(i * rows, rows) for i in range(3))
    copies = [
        pltpu.make_async_copy(source, target, sems.at[i])
        for i, (source, target) in enumerate(
            (
                (k_ref.at[:, other], kv_other.at[first]),
                (v_ref.at[:, other], kv_other.at[second]),
                (k_ref.at[:, other], kvq_other.at[first]),
                (v_ref.at[:, other], kvq_other.at[second]),
                (q_ref.at[:, other], kvq_other.at[third]),
                (k_ref.at[:, own], kv_own.at[first]),
                (v_ref.at[:, own], kv_own.at[second]),
                (q_ref.at[:, own], q_own),
                (q_ref.at[:, other], q_other),
            )
        )
    ]
    for copy in copies:
        copy.start()
    for copy in copies:
        copy.wait()


def attend_kernel(rows, n_keys, *refs):
    kv_refs, rest = refs[:n_keys], refs[n_keys:]
    n_queries = len(rest) // 2
    q_refs, o_refs = rest[:n_queries], rest[n_queries:]
    width = q_refs[0].shape[1]
    scale = 1.0 / math.sqrt(HD)
    lane = lax.broadcasted_iota(jnp.int32, (n_queries * rows, HD), 1)
    stats = jnp.zeros((n_queries * rows, HD), jnp.float32)
    for h in range(width // HD):
        columns = slice(h * HD, (h + 1) * HD)
        q = jnp.concatenate([ref[ref.shape[0] - rows :, columns] for ref in q_refs], axis=0)
        k = jnp.concatenate([ref[:rows, columns] for ref in kv_refs], axis=0)
        v = jnp.concatenate([ref[rows : 2 * rows, columns] for ref in kv_refs], axis=0)
        scores = (
            lax.dot_general(q, k, (((1,), (1,)), ((), ())), preferred_element_type=jnp.float32)
            * scale
        )
        top = jnp.max(scores, axis=1, keepdims=True)
        weights = jnp.exp(scores - top)
        total = jnp.sum(weights, axis=1, keepdims=True)
        mixed = jnp.dot(weights.astype(jnp.bfloat16), v, preferred_element_type=jnp.float32)
        mixed = mixed.astype(jnp.bfloat16)
        for i, term in enumerate(terms(top, 3) + terms(total, 2)):
            stats = jnp.where(lane == i * GAP + h, term, stats)
        for i, ref in enumerate(o_refs):
            ref[:, columns] = mixed[i * rows : (i + 1) * rows]
    stats = stats.astype(jnp.bfloat16)
    for i, ref in enumerate(o_refs):
        ref[:, width:] = stats[i * rows : (i + 1) * rows]


def merge_kernel(members, *refs):
    pieces, out_ref = refs[:-1], refs[-1]
    width = pieces[0].shape[1] - HD
    half = lax.rem(lax.axis_index("blk"), 2)
    for which, group in ((half, pieces[:members]), (1 - half, pieces[members:])):
        tops, totals = [], []
        for ref in group:
            stats = ref[:, width:].astype(jnp.float32)
            shifted = [stats] + [pltpu.roll(stats, HD - i * GAP, 1) for i in range(1, PARTS)]
            tops.append(shifted[0] + shifted[1] + shifted[2])
            totals.append(shifted[3] + shifted[4])
        common = tops[0]
        for top in tops[1:]:
            common = jnp.maximum(common, top)
        factors = [jnp.exp(top - common) for top in tops]
        row_sum = sum(f * t for f, t in zip(factors, totals))
        factors = [f / row_sum for f in factors]
        for h in range(width // HD):
            columns = slice(h * HD, (h + 1) * HD)
            mixed = sum(
                f[:, h : h + 1] * ref[:, columns].astype(jnp.float32)
                for f, ref in zip(factors, group)
            )
            target = pl.multiple_of(which * width + h * HD, HD)
            out_ref[:, pl.ds(target, HD)] = mixed.astype(out_ref.dtype)


def paired(queries, key_rows, value_rows):
    rows = queries.shape[0]
    width = queries.shape[1] // 2
    planes, members = lax.axis_size("blk"), lax.axis_size("team")

    def shape(n_rows, columns):
        return jax.ShapeDtypeStruct((n_rows, columns), queries.dtype)

    def send(array, plane_bits, turn):
        pairs = [
            (z * members + m, (z ^ plane_bits) * members + (m + turn) % members)
            for z in range(planes)
            for m in range(members)
        ]
        return lax.ppermute(array, ("blk", "team"), pairs)

    kv_own, kv_other, kvq_other, q_own, q_other = pl.pallas_call(
        partial(pack_kernel, width),
        out_shape=[
            shape(2 * rows, width),
            shape(2 * rows, width),
            shape(3 * rows, width),
            shape(rows, width),
            shape(rows, width),
        ],
        in_specs=[pl.BlockSpec(memory_space=pltpu.HBM)] * 3,
        out_specs=[vmem_spec()] * 5,
        scratch_shapes=[pltpu.SemaphoreType.DMA((9,))],
        compiler_params=params(),
        name="pack",
    )(hbm_array(queries), hbm_array(key_rows), hbm_array(value_rows))

    far = {}
    for p in [planes - 1, 1] + list(range(planes - 2, 1, -1)):
        far[p] = send(kvq_other if p == 1 else (kv_other if p % 2 else kv_own), p, 0)
    keys = [kv_own] + [far[p] for p in range(1, planes)]
    asked = [q_own, far[1]]
    for m in range(1, members):
        asked += [send(q_own, 0, m), send(q_other, 1, m)]
    answers = pl.pallas_call(
        partial(attend_kernel, rows, planes),
        out_shape=[shape(rows, width + HD)] * len(asked),
        in_specs=[vmem_spec()] * (planes + len(asked)),
        out_specs=[vmem_spec()] * len(asked),
        compiler_params=params(),
        name="attend",
    )(*keys, *asked)
    own_half, other_half = [answers[0]], []
    for m in reversed(range(1, members)):
        other_half.append(send(answers[2 * m + 1], 1, members - m))
        own_half.append(send(answers[2 * m], 0, members - m))
    other_half.append(send(answers[1], 1, 0))
    return pl.pallas_call(
        partial(merge_kernel, members),
        out_shape=shape(rows, 2 * width),
        in_specs=[vmem_spec()] * (2 * members),
        out_specs=vmem_spec(),
        compiler_params=params(),
        name="merge",
    )(*own_half, *other_half)


def solution(mesh):
    spec = P(("groups", "blk", "team"), "head")
    planes = mesh.shape["blk"]

    def local(queries, key_rows, value_rows):
        heads = queries.shape[1] // HD
        pairs_up = planes > 1 and planes & (planes - 1) == 0 and heads % 2 == 0 and heads // 2 <= GAP
        plan = paired if pairs_up else gathered
        return plan(queries, key_rows, value_rows)

    return jax.shard_map(
        local, mesh=mesh, in_specs=(spec,) * 3, out_specs=spec, check_vma=False
    )
```

```python
from functools import partial
import math

import jax
import jax.numpy as jnp
from jax import lax
from jax.experimental import pallas as pl
from jax.experimental.pallas import tpu as pltpu
from jax.sharding import PartitionSpec as P


HD = 128
T_DEV = 48


def attend_block(running, key_block, value_block, query_rows, score_scale):
    row_top, row_total, weighted = running
    scores = (
        jnp.einsum("qhd,khd->qhk", query_rows, key_block, preferred_element_type=jnp.float32)
        * score_scale
    )
    new_top = jnp.maximum(row_top, jnp.max(scores, axis=2))
    shrink = jnp.exp(row_top - new_top)
    weights = jnp.exp(scores - new_top[:, :, None])
    row_total = row_total * shrink + jnp.sum(weights, axis=2)
    weighted = weighted * shrink[:, :, None] + jnp.einsum(
        "qhk,khd->qhd",
        weights.astype(jnp.bfloat16),
        value_block,
        preferred_element_type=jnp.float32,
    )
    return (new_top, row_total, weighted)


def fold_piece(running, shard_piece, query_rows, score_scale):
    key_piece, value_piece = shard_piece
    piece_rows = key_piece.shape[0]
    block_rows = T_DEV
    local_heads = query_rows.shape[1]
    key_blocks = key_piece.reshape(piece_rows // block_rows, block_rows, local_heads, HD)
    value_blocks = value_piece.reshape(piece_rows // block_rows, block_rows, local_heads, HD)

    def one_block(current, block_pair):
        return (attend_block(current, block_pair[0], block_pair[1], query_rows, score_scale), None)

    running, _ = lax.scan(one_block, running, (key_blocks, value_blocks))
    return running


def gathered(queries, key_rows, value_rows):
    own_rows = queries.shape[0]
    local_heads = queries.shape[1] // HD
    score_scale = 1.0 / math.sqrt(HD)
    team_queries = lax.all_gather(queries, "team", axis=0, tiled=True)
    team_count = team_queries.shape[0]
    query_heads = team_queries.reshape(team_count, local_heads, HD)
    folder = partial(fold_piece, query_rows=query_heads, score_scale=score_scale)
    row_top, row_total, weighted = folder(
        (
            jnp.full((team_count, local_heads), -1e30, jnp.float32),
            jnp.zeros((team_count, local_heads), jnp.float32),
            jnp.zeros((team_count, local_heads, HD), jnp.float32),
        ),
        (
            lax.all_gather(key_rows, "blk", axis=0, tiled=True),
            lax.all_gather(value_rows, "blk", axis=0, tiled=True),
        ),
    )
    swapped, member_tops, totals = (
        lax.all_to_all(
            weighted.reshape(team_count, local_heads * HD),
            "team",
            split_axis=0,
            concat_axis=0,
            tiled=True,
        ),
        lax.all_to_all(row_top, "team", split_axis=0, concat_axis=0, tiled=True),
        lax.all_to_all(row_total, "team", split_axis=0, concat_axis=0, tiled=True),
    )
    members = lax.axis_size("team")
    member_tops = member_tops.reshape(members, own_rows, local_heads)
    common_top = jnp.max(member_tops, axis=0)
    factor = jnp.exp(member_tops - common_top[None])
    row_sum = jnp.sum(factor * totals.reshape(members, own_rows, local_heads), axis=0)
    summed = jnp.sum(
        factor[:, :, :, None] * swapped.reshape(members, own_rows, local_heads, HD), axis=0
    )
    mixed_rows = summed / row_sum[:, :, None]
    return mixed_rows.reshape(own_rows, local_heads * HD).astype(jnp.bfloat16)


TOPS, PARTS = 3, 5
GAP = 128 // 8


def vmem_spec():
    return pl.BlockSpec(memory_space=pltpu.VMEM)


def hbm_array(array):
    return pltpu.with_memory_space_constraint(array, pltpu.HBM)


def params():
    return pltpu.CompilerParams(vmem_limit_bytes=16 * 2**20)


def pack_kernel(width, pieces, *refs):
    n_outs = len(pieces)
    sems = refs[-1]
    args, outs = refs[: -1 - n_outs], refs[-1 - n_outs : -1]
    rows = args[0].shape[0]
    own = lax.rem(lax.axis_index("team"), 2)
    halves = [pl.ds(pl.multiple_of(h * width, HD), width) for h in (own, 1 - own)]
    copies = []
    for parts, out in zip(pieces, outs):
        for i, (arg, half) in enumerate(parts):
            source = args[arg].at[:, halves[half]]
            target = out.at[pl.ds(i * rows, rows)]
            copies.append(pltpu.make_async_copy(source, target, sems.at[len(copies)]))
            copies[-1].start()
    for copy in copies:
        copy.wait()


def pack(pieces, *arrays):
    rows, width = arrays[0].shape[0], arrays[0].shape[1] // 2
    return pl.pallas_call(
        partial(pack_kernel, width, pieces),
        out_shape=[
            jax.ShapeDtypeStruct((len(parts) * rows, width), arrays[0].dtype) for parts in pieces
        ],
        in_specs=[pl.BlockSpec(memory_space=pltpu.HBM)] * len(arrays),
        out_specs=[vmem_spec()] * len(pieces),
        scratch_shapes=[pltpu.SemaphoreType.DMA((sum(map(len, pieces)),))],
        compiler_params=params(),
        name="pack",
    )(*map(hbm_array, arrays))


def attend_kernel(rows, n_keys, *refs):
    kv_refs, rest = refs[:n_keys], refs[n_keys:]
    n_queries = len(rest) // 2
    q_refs, o_refs = rest[:n_queries], rest[n_queries:]
    width = q_refs[0].shape[1]
    scale = 1.0 / math.sqrt(HD)
    lane = lax.broadcasted_iota(jnp.int32, (n_queries * rows, HD), 1)
    slot, part = lax.rem(lane, GAP), lax.div(lane, GAP)
    stats = jnp.zeros((n_queries * rows, HD), jnp.float32)
    for h in range(width // HD):
        columns = slice(h * HD, (h + 1) * HD)
        q = jnp.concatenate([ref[ref.shape[0] - rows :, columns] for ref in q_refs], axis=0)
        k = jnp.concatenate([ref[:rows, columns] for ref in kv_refs], axis=0)
        v = jnp.concatenate([ref[rows : 2 * rows, columns] for ref in kv_refs], axis=0)
        scores = (
            lax.dot_general(q, k, (((1,), (1,)), ((), ())), preferred_element_type=jnp.float32)
            * scale
        )
        top = jnp.max(scores, axis=1, keepdims=True)
        weights = jnp.exp(scores - top)
        total = jnp.sum(weights, axis=1, keepdims=True)
        mixed = jnp.dot(weights.astype(jnp.bfloat16), v, preferred_element_type=jnp.float32)
        mixed = mixed.astype(jnp.bfloat16)
        stats = jnp.where(slot == h, jnp.where(part < TOPS, top, total), stats)
        for i, ref in enumerate(o_refs):
            ref[:, columns] = mixed[i * rows : (i + 1) * rows]
    first = stats.astype(jnp.bfloat16).astype(jnp.float32)
    left = stats - first
    second = left.astype(jnp.bfloat16).astype(jnp.float32)
    is_second = (part == 1) | (part == TOPS + 1)
    stats = jnp.where(is_second, second, jnp.where(part == 2, left - second, first))
    stats = stats.astype(jnp.bfloat16)
    for i, ref in enumerate(o_refs):
        ref[:, width:] = stats[i * rows : (i + 1) * rows]


def merge_kernel(*refs):
    pieces, out_ref = refs[:-1], refs[-1]
    width = pieces[0].shape[1] - HD
    tops, totals = [], []
    for ref in pieces:
        stats = ref[:, width:].astype(jnp.float32)
        shifted = [stats] + [pltpu.roll(stats, HD - i * GAP, 1) for i in range(1, PARTS)]
        tops.append(shifted[0] + shifted[1] + shifted[2])
        totals.append(shifted[3] + shifted[4])
    common = tops[0]
    for top in tops[1:]:
        common = jnp.maximum(common, top)
    factors = [jnp.exp(top - common) for top in tops]
    row_sum = sum(f * t for f, t in zip(factors, totals))
    factors = [f / row_sum for f in factors]
    for h in range(width // HD):
        columns = slice(h * HD, (h + 1) * HD)
        mixed = sum(
            f[:, h : h + 1] * ref[:, columns].astype(jnp.float32) for f, ref in zip(factors, pieces)
        )
        out_ref[:, columns] = mixed.astype(out_ref.dtype)


def finish_kernel(other_ref, own_ref, answer_ref, out_ref, own_half, sems):
    width = other_ref.shape[1]
    half = lax.rem(lax.axis_index("team"), 2)
    copies = [
        pltpu.make_async_copy(
            source, out_ref.at[:, pl.ds(pl.multiple_of(which * width, HD), width)], sems.at[i]
        )
        for i, (source, which) in enumerate(((other_ref, 1 - half), (own_half, half)))
    ]
    copies[0].start()
    merge_kernel(own_ref, answer_ref, own_half)
    copies[1].start()
    for copy in copies:
        copy.wait()


def paired(queries, key_rows, value_rows):
    rows = queries.shape[0]
    width = queries.shape[1] // 2
    planes, members = lax.axis_size("blk"), lax.axis_size("team")

    def shape(n_rows, columns):
        return jax.ShapeDtypeStruct((n_rows, columns), queries.dtype)

    def send(array, plane_bits, member_bits):
        pairs = [
            (z * members + m, (z ^ plane_bits) * members + (m ^ member_bits))
            for z in range(planes)
            for m in range(members)
        ]
        return lax.ppermute(array, ("blk", "team"), pairs)

    kv_own, kv_other, kvq_other, q_own, q_other = pack(
        (
            ((0, 0), (1, 0)),
            ((0, 1), (1, 1)),
            ((0, 1), (1, 1), (2, 1)),
            ((2, 0),),
            ((2, 1),),
        ),
        key_rows,
        value_rows,
        queries,
    )

    near = send(kvq_other, 0, 1)
    keys = [kv_own, near]
    for plane_bits, member_bits in key_sends(planes, members):
        array = kv_other if member_bits % 2 else kv_own
        keys.append(send(array, plane_bits, member_bits))
    asked = [q_own, near, send(q_own, 1, 0), send(q_other, 1, 1)]
    own, *answers = pl.pallas_call(
        partial(attend_kernel, rows, len(keys)),
        out_shape=[shape(rows, width + HD)] * len(asked),
        in_specs=[vmem_spec()] * (len(keys) + len(asked)),
        out_specs=[vmem_spec()] * len(asked),
        compiler_params=params(),
        name="attend",
    )(*keys, *asked)
    back_near = send(answers[0], 0, 1)
    back_ask = send(answers[1], 1, 0)
    back_cross = send(answers[2], 1, 1)
    early = pl.pallas_call(
        merge_kernel,
        out_shape=shape(rows, width),
        in_specs=[vmem_spec()] * 2,
        out_specs=vmem_spec(),
        compiler_params=params(),
        name="merge",
    )(back_near, back_cross)
    return pl.pallas_call(
        finish_kernel,
        out_shape=shape(rows, 2 * width),
        in_specs=[vmem_spec()] * 3,
        out_specs=pl.BlockSpec(memory_space=pl.ANY),
        scratch_shapes=[pltpu.VMEM((rows, width), queries.dtype), pltpu.SemaphoreType.DMA((2,))],
        compiler_params=params(),
        name="finish",
    )(early, own, back_ask)


def key_sends(planes, members):
    return [(p, m) for p in range(0, planes, 2) for m in range(members) if p or m > 1]


def solution(mesh):
    spec = P(("groups", "blk", "team"), "head")
    planes, members = mesh.shape["blk"], mesh.shape["team"]
    in_quads = all(n > 1 and n & (n - 1) == 0 for n in (planes, members))

    def local(queries, key_rows, value_rows):
        heads = queries.shape[1] // HD
        plan = paired if in_quads and heads % 2 == 0 and heads // 2 <= GAP else gathered
        return plan(queries, key_rows, value_rows)

    return jax.shard_map(local, mesh=mesh, in_specs=(spec,) * 3, out_specs=spec, check_vma=False)
```

```python
from functools import partial
import math

import jax
import jax.numpy as jnp
from jax import lax
from jax.experimental import pallas as pl
from jax.experimental.pallas import tpu as pltpu
from jax.sharding import PartitionSpec as P


HD = 128
T_DEV = 48


def attend_block(running, key_block, value_block, query_rows, score_scale):
    row_top, row_total, weighted = running
    scores = (
        jnp.einsum("qhd,khd->qhk", query_rows, key_block, preferred_element_type=jnp.float32)
        * score_scale
    )
    new_top = jnp.maximum(row_top, jnp.max(scores, axis=2))
    shrink = jnp.exp(row_top - new_top)
    weights = jnp.exp(scores - new_top[:, :, None])
    row_total = row_total * shrink + jnp.sum(weights, axis=2)
    weighted = weighted * shrink[:, :, None] + jnp.einsum(
        "qhk,khd->qhd",
        weights.astype(jnp.bfloat16),
        value_block,
        preferred_element_type=jnp.float32,
    )
    return (new_top, row_total, weighted)


def fold_piece(running, shard_piece, query_rows, score_scale):
    key_piece, value_piece = shard_piece
    piece_rows = key_piece.shape[0]
    block_rows = T_DEV
    local_heads = query_rows.shape[1]
    key_blocks = key_piece.reshape(piece_rows // block_rows, block_rows, local_heads, HD)
    value_blocks = value_piece.reshape(piece_rows // block_rows, block_rows, local_heads, HD)

    def one_block(current, block_pair):
        return (attend_block(current, block_pair[0], block_pair[1], query_rows, score_scale), None)

    running, _ = lax.scan(one_block, running, (key_blocks, value_blocks))
    return running


def gathered(queries, key_rows, value_rows):
    own_rows = queries.shape[0]
    local_heads = queries.shape[1] // HD
    score_scale = 1.0 / math.sqrt(HD)
    team_queries = lax.all_gather(queries, "team", axis=0, tiled=True)
    team_count = team_queries.shape[0]
    query_heads = team_queries.reshape(team_count, local_heads, HD)
    folder = partial(fold_piece, query_rows=query_heads, score_scale=score_scale)
    row_top, row_total, weighted = folder(
        (
            jnp.full((team_count, local_heads), -1e30, jnp.float32),
            jnp.zeros((team_count, local_heads), jnp.float32),
            jnp.zeros((team_count, local_heads, HD), jnp.float32),
        ),
        (
            lax.all_gather(key_rows, "blk", axis=0, tiled=True),
            lax.all_gather(value_rows, "blk", axis=0, tiled=True),
        ),
    )
    swapped, member_tops, totals = (
        lax.all_to_all(
            weighted.reshape(team_count, local_heads * HD),
            "team",
            split_axis=0,
            concat_axis=0,
            tiled=True,
        ),
        lax.all_to_all(row_top, "team", split_axis=0, concat_axis=0, tiled=True),
        lax.all_to_all(row_total, "team", split_axis=0, concat_axis=0, tiled=True),
    )
    members = lax.axis_size("team")
    member_tops = member_tops.reshape(members, own_rows, local_heads)
    common_top = jnp.max(member_tops, axis=0)
    factor = jnp.exp(member_tops - common_top[None])
    row_sum = jnp.sum(factor * totals.reshape(members, own_rows, local_heads), axis=0)
    summed = jnp.sum(
        factor[:, :, :, None] * swapped.reshape(members, own_rows, local_heads, HD), axis=0
    )
    mixed_rows = summed / row_sum[:, :, None]
    return mixed_rows.reshape(own_rows, local_heads * HD).astype(jnp.bfloat16)


TOPS, PARTS = 3, 5
GAP = 128 // 8


def vmem_spec():
    return pl.BlockSpec(memory_space=pltpu.VMEM)


def hbm_array(array):
    return pltpu.with_memory_space_constraint(array, pltpu.HBM)


def params():
    return pltpu.CompilerParams(vmem_limit_bytes=16 * 2**20)


def pack_kernel(width, pieces, *refs):
    n_outs = len(pieces)
    sems = refs[-1]
    args, outs = refs[: -1 - n_outs], refs[-1 - n_outs : -1]
    rows = args[0].shape[0]
    own = lax.rem(lax.axis_index("team"), 2)
    halves = [pl.ds(pl.multiple_of(h * width, HD), width) for h in (own, 1 - own)]
    copies = []
    for parts, out in zip(pieces, outs):
        for i, (arg, half) in enumerate(parts):
            source = args[arg].at[:, halves[half]]
            target = out.at[pl.ds(i * rows, rows)]
            copies.append(pltpu.make_async_copy(source, target, sems.at[len(copies)]))
            copies[-1].start()
    for copy in copies:
        copy.wait()


def pack(pieces, *arrays):
    rows, width = arrays[0].shape[0], arrays[0].shape[1] // 2
    return pl.pallas_call(
        partial(pack_kernel, width, pieces),
        out_shape=[
            jax.ShapeDtypeStruct((len(parts) * rows, width), arrays[0].dtype) for parts in pieces
        ],
        in_specs=[pl.BlockSpec(memory_space=pltpu.HBM)] * len(arrays),
        out_specs=[vmem_spec()] * len(pieces),
        scratch_shapes=[pltpu.SemaphoreType.DMA((sum(map(len, pieces)),))],
        compiler_params=params(),
        name="pack",
    )(*map(hbm_array, arrays))


def attend_kernel(rows, n_keys, *refs):
    kv_refs, rest = refs[:n_keys], refs[n_keys:]
    n_queries = len(rest) // 2
    q_refs, o_refs = rest[:n_queries], rest[n_queries:]
    width = q_refs[0].shape[1]
    scale = math.log2(math.e) / math.sqrt(HD)
    lane = lax.broadcasted_iota(jnp.int32, (n_queries * rows, HD), 1)
    slot, part = lax.rem(lane, GAP), lax.div(lane, GAP)
    stats = jnp.zeros((n_queries * rows, HD), jnp.float32)

    def load(refs, low, h):
        columns = slice(h * HD, (h + 1) * HD)
        return jnp.concatenate([r[low(r) : low(r) + rows, columns] for r in refs], axis=0)

    def score(h):
        q = load(q_refs, lambda r: r.shape[0] - rows, h)
        k = load(kv_refs, lambda r: 0, h)
        product = lax.dot_general(
            q, k, (((1,), (1,)), ((), ())), preferred_element_type=jnp.float32
        )
        return product * scale

    def weigh(scores):
        top = jnp.max(scores, axis=1, keepdims=True)
        return top, jnp.exp2(scores - top).astype(jnp.bfloat16)

    def mix(h, top, weights, stats):
        v = load(kv_refs, lambda r: rows, h)
        v = jnp.concatenate([v, jnp.ones_like(v)], axis=1)
        mixed = jnp.dot(weights, v, preferred_element_type=jnp.float32)
        for i, ref in enumerate(o_refs):
            ref[:, h * HD : (h + 1) * HD] = mixed[i * rows : (i + 1) * rows, :HD].astype(ref.dtype)
        return jnp.where(slot == h, jnp.where(part < TOPS, top, mixed[:, HD:]), stats)

    heads = width // HD
    scores = [score(h) for h in range(heads)]
    pairs = [weigh(s) for s in scores]
    for h, (top, weights) in enumerate(pairs):
        stats = mix(h, top, weights, stats)
    first = stats.astype(jnp.bfloat16).astype(jnp.float32)
    left = stats - first
    second = left.astype(jnp.bfloat16).astype(jnp.float32)
    is_second = (part == 1) | (part == TOPS + 1)
    stats = jnp.where(is_second, second, jnp.where(part == 2, left - second, first))
    stats = stats.astype(jnp.bfloat16)
    for i, ref in enumerate(o_refs):
        ref[:, width:] = stats[i * rows : (i + 1) * rows]


def merge_kernel(*refs):
    pieces, out_ref = refs[:-1], refs[-1]
    width = pieces[0].shape[1] - HD
    tops, totals = [], []
    for ref in pieces:
        stats = ref[:, width:].astype(jnp.float32)
        shifted = [stats] + [pltpu.roll(stats, HD - i * GAP, 1) for i in range(1, PARTS)]
        tops.append(shifted[0] + shifted[1] + shifted[2])
        totals.append(shifted[3] + shifted[4])
    common = tops[0]
    for top in tops[1:]:
        common = jnp.maximum(common, top)
    factors = [jnp.exp2(top - common) for top in tops]
    row_sum = sum(f * t for f, t in zip(factors, totals))
    factors = [f / row_sum for f in factors]
    for h in range(width // HD):
        columns = slice(h * HD, (h + 1) * HD)
        mixed = sum(
            f[:, h : h + 1] * ref[:, columns].astype(jnp.float32) for f, ref in zip(factors, pieces)
        )
        out_ref[:, columns] = mixed.astype(out_ref.dtype)


def finish_kernel(other_ref, own_ref, answer_ref, out_ref, own_half, sems):
    width = other_ref.shape[1]
    half = lax.rem(lax.axis_index("team"), 2)
    copies = [
        pltpu.make_async_copy(
            source, out_ref.at[:, pl.ds(pl.multiple_of(which * width, HD), width)], sems.at[i]
        )
        for i, (source, which) in enumerate(((other_ref, 1 - half), (own_half, half)))
    ]
    copies[0].start()
    merge_kernel(own_ref, answer_ref, own_half)
    copies[1].start()
    for copy in copies:
        copy.wait()


def paired(queries, key_rows, value_rows):
    rows = queries.shape[0]
    width = queries.shape[1] // 2
    planes, members = lax.axis_size("blk"), lax.axis_size("team")

    def shape(n_rows, columns):
        return jax.ShapeDtypeStruct((n_rows, columns), queries.dtype)

    def send(array, plane_bits, member_bits):
        pairs = [
            (z * members + m, (z ^ plane_bits) * members + (m ^ member_bits))
            for z in range(planes)
            for m in range(members)
        ]
        return lax.ppermute(array, ("blk", "team"), pairs)

    kv_own, kv_other, kvq_other, q_own, q_other = pack(
        (
            ((0, 0), (1, 0)),
            ((0, 1), (1, 1)),
            ((0, 1), (1, 1), (2, 1)),
            ((2, 0),),
            ((2, 1),),
        ),
        key_rows,
        value_rows,
        queries,
    )

    near = send(kvq_other, 0, 1)
    keys = [kv_own, near]
    for plane_bits, member_bits in key_sends(planes, members):
        array = kv_other if member_bits % 2 else kv_own
        keys.append(send(array, plane_bits, member_bits))
    asked = [q_own, near, send(q_own, 1, 0), send(q_other, 1, 1)]
    own, *answers = pl.pallas_call(
        partial(attend_kernel, rows, len(keys)),
        out_shape=[shape(rows, width + HD)] * len(asked),
        in_specs=[vmem_spec()] * (len(keys) + len(asked)),
        out_specs=[vmem_spec()] * len(asked),
        compiler_params=params(),
        name="attend",
    )(*keys, *asked)
    back_near = send(answers[0], 0, 1)
    back_ask = send(answers[1], 1, 0)
    back_cross = send(answers[2], 1, 1)
    early = pl.pallas_call(
        merge_kernel,
        out_shape=shape(rows, width),
        in_specs=[vmem_spec()] * 2,
        out_specs=vmem_spec(),
        compiler_params=params(),
        name="merge",
    )(back_near, back_cross)
    return pl.pallas_call(
        finish_kernel,
        out_shape=shape(rows, 2 * width),
        in_specs=[vmem_spec()] * 3,
        out_specs=pl.BlockSpec(memory_space=pl.ANY),
        scratch_shapes=[pltpu.VMEM((rows, width), queries.dtype), pltpu.SemaphoreType.DMA((2,))],
        compiler_params=params(),
        name="finish",
    )(early, own, back_ask)


def key_sends(planes, members):
    return [(p, m) for p in range(0, planes, 2) for m in range(members) if p or m > 1]


def solution(mesh):
    spec = P(("groups", "blk", "team"), "head")
    planes, members = mesh.shape["blk"], mesh.shape["team"]
    in_quads = all(n > 1 and n & (n - 1) == 0 for n in (planes, members))

    def local(queries, key_rows, value_rows):
        heads = queries.shape[1] // HD
        plan = paired if in_quads and heads % 2 == 0 and heads // 2 <= GAP else gathered
        return plan(queries, key_rows, value_rows)

    return jax.shard_map(local, mesh=mesh, in_specs=(spec,) * 3, out_specs=spec, check_vma=False)
```

```python
from functools import partial
import math

import jax
import jax.numpy as jnp
from jax import lax
from jax.experimental import pallas as pl
from jax.experimental.pallas import tpu as pltpu
from jax.sharding import PartitionSpec as P


HD = 128
T_DEV = 48


def attend_block(running, key_block, value_block, query_rows, score_scale):
    row_top, row_total, weighted = running
    scores = (
        jnp.einsum("qhd,khd->qhk", query_rows, key_block, preferred_element_type=jnp.float32)
        * score_scale
    )
    new_top = jnp.maximum(row_top, jnp.max(scores, axis=2))
    shrink = jnp.exp(row_top - new_top)
    weights = jnp.exp(scores - new_top[:, :, None])
    row_total = row_total * shrink + jnp.sum(weights, axis=2)
    weighted = weighted * shrink[:, :, None] + jnp.einsum(
        "qhk,khd->qhd",
        weights.astype(jnp.bfloat16),
        value_block,
        preferred_element_type=jnp.float32,
    )
    return (new_top, row_total, weighted)


def fold_piece(running, shard_piece, query_rows, score_scale):
    key_piece, value_piece = shard_piece
    piece_rows = key_piece.shape[0]
    block_rows = T_DEV
    local_heads = query_rows.shape[1]
    key_blocks = key_piece.reshape(piece_rows // block_rows, block_rows, local_heads, HD)
    value_blocks = value_piece.reshape(piece_rows // block_rows, block_rows, local_heads, HD)

    def one_block(current, block_pair):
        return (attend_block(current, block_pair[0], block_pair[1], query_rows, score_scale), None)

    running, _ = lax.scan(one_block, running, (key_blocks, value_blocks))
    return running


def gathered(queries, key_rows, value_rows):
    own_rows = queries.shape[0]
    local_heads = queries.shape[1] // HD
    score_scale = 1.0 / math.sqrt(HD)
    team_queries = lax.all_gather(queries, "team", axis=0, tiled=True)
    team_count = team_queries.shape[0]
    query_heads = team_queries.reshape(team_count, local_heads, HD)
    folder = partial(fold_piece, query_rows=query_heads, score_scale=score_scale)
    row_top, row_total, weighted = folder(
        (
            jnp.full((team_count, local_heads), -1e30, jnp.float32),
            jnp.zeros((team_count, local_heads), jnp.float32),
            jnp.zeros((team_count, local_heads, HD), jnp.float32),
        ),
        (
            lax.all_gather(key_rows, "blk", axis=0, tiled=True),
            lax.all_gather(value_rows, "blk", axis=0, tiled=True),
        ),
    )
    swapped, member_tops, totals = (
        lax.all_to_all(
            weighted.reshape(team_count, local_heads * HD),
            "team",
            split_axis=0,
            concat_axis=0,
            tiled=True,
        ),
        lax.all_to_all(row_top, "team", split_axis=0, concat_axis=0, tiled=True),
        lax.all_to_all(row_total, "team", split_axis=0, concat_axis=0, tiled=True),
    )
    members = lax.axis_size("team")
    member_tops = member_tops.reshape(members, own_rows, local_heads)
    common_top = jnp.max(member_tops, axis=0)
    factor = jnp.exp(member_tops - common_top[None])
    row_sum = jnp.sum(factor * totals.reshape(members, own_rows, local_heads), axis=0)
    summed = jnp.sum(
        factor[:, :, :, None] * swapped.reshape(members, own_rows, local_heads, HD), axis=0
    )
    mixed_rows = summed / row_sum[:, :, None]
    return mixed_rows.reshape(own_rows, local_heads * HD).astype(jnp.bfloat16)


TOPS, PARTS = 3, 5
GAP = 128 // 8


def vmem_spec():
    return pl.BlockSpec(memory_space=pltpu.VMEM)


def hbm_array(array):
    return pltpu.with_memory_space_constraint(array, pltpu.HBM)


def params():
    return pltpu.CompilerParams(vmem_limit_bytes=16 * 2**20)


def pack_kernel(width, pieces, *refs):
    n_outs = len(pieces)
    sems = refs[-1]
    args, outs = refs[: -1 - n_outs], refs[-1 - n_outs : -1]
    rows = args[0].shape[0]
    own = lax.rem(lax.axis_index("team"), 2)
    halves = [pl.ds(pl.multiple_of(h * width, HD), width) for h in (own, 1 - own)]
    copies = []
    for parts, out in zip(pieces, outs):
        for i, (arg, half) in enumerate(parts):
            source = args[arg].at[:, halves[half]]
            target = out.at[pl.ds(i * rows, rows)]
            copies.append(pltpu.make_async_copy(source, target, sems.at[len(copies)]))
            copies[-1].start()
    for copy in copies:
        copy.wait()


def pack(pieces, *arrays):
    rows, width = arrays[0].shape[0], arrays[0].shape[1] // 2
    return pl.pallas_call(
        partial(pack_kernel, width, pieces),
        out_shape=[
            jax.ShapeDtypeStruct((len(parts) * rows, width), arrays[0].dtype) for parts in pieces
        ],
        in_specs=[pl.BlockSpec(memory_space=pltpu.HBM)] * len(arrays),
        out_specs=[vmem_spec()] * len(pieces),
        scratch_shapes=[pltpu.SemaphoreType.DMA((sum(map(len, pieces)),))],
        compiler_params=params(),
        name="pack",
    )(*map(hbm_array, arrays))


def attend_kernel(rows, k_at, v_at, q_at, *refs):
    o_refs = refs[-len(q_at) :]
    width = o_refs[0].shape[1] - HD
    scale = math.log2(math.e) / math.sqrt(HD)
    lane = lax.broadcasted_iota(jnp.int32, (len(q_at) * rows, HD), 1)
    slot, part = lax.rem(lane, GAP), lax.div(lane, GAP)
    stats = jnp.zeros(lane.shape, jnp.float32)

    def load(places, h):
        columns = slice(h * HD, (h + 1) * HD)
        return jnp.concatenate([refs[i][row : row + rows, columns] for i, row in places], axis=0)

    def score(h):
        q, k = load(q_at, h), load(k_at, h)
        product = lax.dot_general(
            q, k, (((1,), (1,)), ((), ())), preferred_element_type=jnp.float32
        )
        return product * scale

    def weigh(scores):
        top = jnp.max(scores, axis=1, keepdims=True)
        return top, jnp.exp2(scores - top).astype(jnp.bfloat16)

    def mix(h, top, weights, stats):
        v = load(v_at, h)
        v = jnp.concatenate([v, jnp.ones_like(v)], axis=1)
        mixed = jnp.dot(weights, v, preferred_element_type=jnp.float32)
        for i, ref in enumerate(o_refs):
            ref[:, h * HD : (h + 1) * HD] = mixed[i * rows : (i + 1) * rows, :HD].astype(ref.dtype)
        return jnp.where(slot == h, jnp.where(part < TOPS, top, mixed[:, HD:]), stats)

    heads = width // HD
    scores = [score(h) for h in range(heads)]
    pairs = [weigh(s) for s in scores]
    for h, (top, weights) in enumerate(pairs):
        stats = mix(h, top, weights, stats)
    first = stats.astype(jnp.bfloat16).astype(jnp.float32)
    left = stats - first
    second = left.astype(jnp.bfloat16).astype(jnp.float32)
    is_second = (part == 1) | (part == TOPS + 1)
    stats = jnp.where(is_second, second, jnp.where(part == 2, left - second, first))
    stats = stats.astype(jnp.bfloat16)
    for i, ref in enumerate(o_refs):
        ref[:, width:] = stats[i * rows : (i + 1) * rows]


def split_kernel(*refs):
    n_others = sum(ref.shape[1] == refs[-1].shape[1] for ref in refs) - 2
    whole_refs, (keys_ref, queries_ref, *other_refs) = refs[: -2 - n_others], refs[-2 - n_others :]
    rows, width = queries_ref.shape
    own = lax.rem(lax.axis_index("team"), 2)
    halves = [pl.ds(pl.multiple_of(half * width, HD), width) for half in (own, 1 - own)]
    queries_ref[...] = whole_refs[-1][:, halves[0]]
    for m, out_ref in enumerate((keys_ref, *other_refs)):
        for i, whole_ref in enumerate(whole_refs[: out_ref.shape[0] // rows]):
            out_ref[i * rows : (i + 1) * rows] = whole_ref[:, halves[m % 2]]


def merge_kernel(*refs):
    pieces, out_ref = refs[:-1], refs[-1]
    width = pieces[0].shape[1] - HD
    tops, totals = [], []
    for ref in pieces:
        stats = ref[:, width:].astype(jnp.float32)
        shifted = [stats] + [pltpu.roll(stats, HD - i * GAP, 1) for i in range(1, PARTS)]
        tops.append(shifted[0] + shifted[1] + shifted[2])
        totals.append(shifted[3] + shifted[4])
    common = tops[0]
    for top in tops[1:]:
        common = jnp.maximum(common, top)
    factors = [jnp.exp2(top - common) for top in tops]
    row_sum = sum(f * t for f, t in zip(factors, totals))
    factors = [f / row_sum for f in factors]
    for h in range(width // HD):
        columns = slice(h * HD, (h + 1) * HD)
        mixed = sum(
            f[:, h : h + 1] * ref[:, columns].astype(jnp.float32) for f, ref in zip(factors, pieces)
        )
        out_ref[:, columns] = mixed.astype(out_ref.dtype)


def finish_kernel(other_ref, own_ref, answer_ref, out_ref, own_half, sems):
    width = other_ref.shape[1]
    half = lax.rem(lax.axis_index("team"), 2)
    copies = [
        pltpu.make_async_copy(
            source, out_ref.at[:, pl.ds(pl.multiple_of(which * width, HD), width)], sems.at[i]
        )
        for i, (source, which) in enumerate(((other_ref, 1 - half), (own_half, half)))
    ]
    copies[0].start()
    merge_kernel(own_ref, answer_ref, own_half)
    copies[1].start()
    for copy in copies:
        copy.wait()


def paired(queries, key_rows, value_rows):
    rows = queries.shape[0]
    width = queries.shape[1] // 2
    planes, members = lax.axis_size("blk"), lax.axis_size("team")

    def shape(n_rows, columns):
        return jax.ShapeDtypeStruct((n_rows, columns), queries.dtype)

    def send(array, plane_bits, member_bits):
        pairs = [
            (z * members + m, (z ^ plane_bits) * members + (m ^ member_bits))
            for z in range(planes)
            for m in range(members)
        ]
        return lax.ppermute(array, ("blk", "team"), pairs)

    far = range(2, planes, 2)
    whole = [send(key_rows, p, 0) for p in far] + [send(queries, 1, 0)]
    kv_own, kvq_other, v_own, v_other, q_own, *kv_other = pack(
        (
            ((0, 0), (1, 0)),
            ((0, 1), (1, 1), (2, 1)),
            ((1, 0),),
            ((1, 1),),
            ((2, 0),),
            *([((0, 1), (1, 1))] if members > 2 else []),
        ),
        key_rows,
        value_rows,
        queries,
    )
    near = send(kvq_other, 0, 1)
    beside = [kv_own, near]
    beside += [send(kv_other[0] if m % 2 else kv_own, 0, m) for m in range(2, members)]
    k_parts, v_parts = [(piece, 0) for piece in beside], [(piece, rows) for piece in beside]
    v_parts += [(send(v_other if m % 2 else v_own, p, m), 0) for p in far for m in range(members)]
    far_rows = len(far) * rows
    mine, asked, *theirs = pl.pallas_call(
        split_kernel,
        out_shape=[shape(max(far_rows, rows), width), shape(rows, width)]
        + [shape(far_rows + (rows if m == 1 else 0), width) for m in range(1, members)],
        in_specs=[vmem_spec()] * len(whole),
        out_specs=[vmem_spec()] * (1 + members),
        compiler_params=params(),
        name="split",
    )(*whole)
    shared = [mine] + [send(theirs[m - 1], 0, m) for m in range(1, members)]
    k_parts += [(piece, i * rows) for piece in shared for i in range(len(far))]
    q_parts = [(q_own, 0), (near, 2 * rows), (asked, 0), (shared[1], far_rows)]
    operands = list({id(piece): piece for piece, _ in k_parts + v_parts + q_parts}.values())
    place = {id(piece): i for i, piece in enumerate(operands)}
    k_at, v_at, q_at = (
        [(place[id(piece)], row) for piece, row in parts] for parts in (k_parts, v_parts, q_parts)
    )
    own, *answers = pl.pallas_call(
        partial(attend_kernel, rows, k_at, v_at, q_at),
        out_shape=[shape(rows, width + HD)] * len(q_at),
        in_specs=[vmem_spec()] * len(operands),
        out_specs=[vmem_spec()] * len(q_at),
        compiler_params=params(),
        name="attend",
    )(*operands)
    back_near = send(answers[0], 0, 1)
    back_ask = send(answers[1], 1, 0)
    back_cross = send(answers[2], 1, 1)
    early = pl.pallas_call(
        merge_kernel,
        out_shape=shape(rows, width),
        in_specs=[vmem_spec()] * 2,
        out_specs=vmem_spec(),
        compiler_params=params(),
        name="merge",
    )(back_near, back_cross)
    return pl.pallas_call(
        finish_kernel,
        out_shape=shape(rows, 2 * width),
        in_specs=[vmem_spec()] * 3,
        out_specs=pl.BlockSpec(memory_space=pl.ANY),
        scratch_shapes=[pltpu.VMEM((rows, width), queries.dtype), pltpu.SemaphoreType.DMA((2,))],
        compiler_params=params(),
        name="finish",
    )(early, own, back_ask)


def solution(mesh):
    spec = P(("groups", "blk", "team"), "head")
    planes, members = mesh.shape["blk"], mesh.shape["team"]
    in_quads = planes > 2 and members > 1 and all(n & (n - 1) == 0 for n in (planes, members))

    def local(queries, key_rows, value_rows):
        heads = queries.shape[1] // HD
        plan = paired if in_quads and heads % 2 == 0 and heads // 2 <= GAP else gathered
        return plan(queries, key_rows, value_rows)

    return jax.shard_map(local, mesh=mesh, in_specs=(spec,) * 3, out_specs=spec, check_vma=False)
```

```python
from functools import partial
import math

import jax
import jax.numpy as jnp
from jax import lax
from jax.experimental import pallas as pl
from jax.experimental.pallas import tpu as pltpu
from jax.sharding import PartitionSpec as P


HD = 128
T_DEV = 48


def attend_block(running, key_block, value_block, query_rows, score_scale):
    row_top, row_total, weighted = running
    scores = (
        jnp.einsum("qhd,khd->qhk", query_rows, key_block, preferred_element_type=jnp.float32)
        * score_scale
    )
    new_top = jnp.maximum(row_top, jnp.max(scores, axis=2))
    shrink = jnp.exp(row_top - new_top)
    weights = jnp.exp(scores - new_top[:, :, None])
    row_total = row_total * shrink + jnp.sum(weights, axis=2)
    weighted = weighted * shrink[:, :, None] + jnp.einsum(
        "qhk,khd->qhd",
        weights.astype(jnp.bfloat16),
        value_block,
        preferred_element_type=jnp.float32,
    )
    return (new_top, row_total, weighted)


def fold_piece(running, shard_piece, query_rows, score_scale):
    key_piece, value_piece = shard_piece
    piece_rows = key_piece.shape[0]
    block_rows = T_DEV
    local_heads = query_rows.shape[1]
    key_blocks = key_piece.reshape(piece_rows // block_rows, block_rows, local_heads, HD)
    value_blocks = value_piece.reshape(piece_rows // block_rows, block_rows, local_heads, HD)

    def one_block(current, block_pair):
        return (attend_block(current, block_pair[0], block_pair[1], query_rows, score_scale), None)

    running, _ = lax.scan(one_block, running, (key_blocks, value_blocks))
    return running


def gathered(queries, key_rows, value_rows):
    own_rows = queries.shape[0]
    local_heads = queries.shape[1] // HD
    score_scale = 1.0 / math.sqrt(HD)
    team_queries = lax.all_gather(queries, "team", axis=0, tiled=True)
    team_count = team_queries.shape[0]
    query_heads = team_queries.reshape(team_count, local_heads, HD)
    folder = partial(fold_piece, query_rows=query_heads, score_scale=score_scale)
    row_top, row_total, weighted = folder(
        (
            jnp.full((team_count, local_heads), -1e30, jnp.float32),
            jnp.zeros((team_count, local_heads), jnp.float32),
            jnp.zeros((team_count, local_heads, HD), jnp.float32),
        ),
        (
            lax.all_gather(key_rows, "blk", axis=0, tiled=True),
            lax.all_gather(value_rows, "blk", axis=0, tiled=True),
        ),
    )
    swapped, member_tops, totals = (
        lax.all_to_all(
            weighted.reshape(team_count, local_heads * HD),
            "team",
            split_axis=0,
            concat_axis=0,
            tiled=True,
        ),
        lax.all_to_all(row_top, "team", split_axis=0, concat_axis=0, tiled=True),
        lax.all_to_all(row_total, "team", split_axis=0, concat_axis=0, tiled=True),
    )
    members = lax.axis_size("team")
    member_tops = member_tops.reshape(members, own_rows, local_heads)
    common_top = jnp.max(member_tops, axis=0)
    factor = jnp.exp(member_tops - common_top[None])
    row_sum = jnp.sum(factor * totals.reshape(members, own_rows, local_heads), axis=0)
    summed = jnp.sum(
        factor[:, :, :, None] * swapped.reshape(members, own_rows, local_heads, HD), axis=0
    )
    mixed_rows = summed / row_sum[:, :, None]
    return mixed_rows.reshape(own_rows, local_heads * HD).astype(jnp.bfloat16)


TOPS, PARTS = 3, 5
GAP = 128 // 8


def vmem_spec():
    return pl.BlockSpec(memory_space=pltpu.VMEM)


def hbm_array(array):
    return pltpu.with_memory_space_constraint(array, pltpu.HBM)


def params():
    return pltpu.CompilerParams(vmem_limit_bytes=16 * 2**20)


def pack_kernel(width, pieces, *refs):
    n_outs = len(pieces)
    sems = refs[-1]
    args, outs = refs[: -1 - n_outs], refs[-1 - n_outs : -1]
    rows = args[0].shape[0]
    own = lax.rem(lax.axis_index("team"), 2)
    halves = [pl.ds(pl.multiple_of(h * width, HD), width) for h in (own, 1 - own)]
    copies = []
    for parts, out in zip(pieces, outs):
        for i, (arg, half) in enumerate(parts):
            source = args[arg].at[:, halves[half]]
            target = out.at[pl.ds(i * rows, rows)]
            copies.append(pltpu.make_async_copy(source, target, sems.at[len(copies)]))
            copies[-1].start()
    for copy in copies:
        copy.wait()


def pack(pieces, *arrays):
    rows, width = arrays[0].shape[0], arrays[0].shape[1] // 2
    return pl.pallas_call(
        partial(pack_kernel, width, pieces),
        out_shape=[
            jax.ShapeDtypeStruct((len(parts) * rows, width), arrays[0].dtype) for parts in pieces
        ],
        in_specs=[pl.BlockSpec(memory_space=pltpu.HBM)] * len(arrays),
        out_specs=[vmem_spec()] * len(pieces),
        scratch_shapes=[pltpu.SemaphoreType.DMA((sum(map(len, pieces)),))],
        compiler_params=params(),
        name="pack",
    )(*map(hbm_array, arrays))


def attend_kernel(rows, k_at, v_at, q_at, *refs):
    o_refs = refs[-len(q_at) :]
    width = o_refs[0].shape[1] - HD
    scale = math.log2(math.e) / math.sqrt(HD)
    lane = lax.broadcasted_iota(jnp.int32, (len(q_at) * rows, HD), 1)
    slot, part = lax.rem(lane, GAP), lax.div(lane, GAP)
    stats = jnp.zeros(lane.shape, jnp.float32)

    def load(places, h):
        columns = slice(h * HD, (h + 1) * HD)
        return jnp.concatenate([refs[i][row : row + rows, columns] for i, row in places], axis=0)

    def score(h):
        q, k = load(q_at, h), load(k_at, h)
        product = lax.dot_general(
            q, k, (((1,), (1,)), ((), ())), preferred_element_type=jnp.float32
        )
        return product * scale

    def weigh(scores):
        top = jnp.max(scores, axis=1, keepdims=True)
        return top, jnp.exp2(scores - top).astype(jnp.bfloat16)

    def mix(h, top, weights, stats):
        v = load(v_at, h)
        v = jnp.concatenate([v, jnp.ones_like(v)], axis=1)
        mixed = jnp.dot(weights, v, preferred_element_type=jnp.float32)
        for i, ref in enumerate(o_refs):
            ref[:, h * HD : (h + 1) * HD] = mixed[i * rows : (i + 1) * rows, :HD].astype(ref.dtype)
        return jnp.where(slot == h, jnp.where(part < TOPS, top, mixed[:, HD:]), stats)

    heads = width // HD
    scores = [score(h) for h in range(heads)]
    pairs = [weigh(s) for s in scores]
    for h, (top, weights) in enumerate(pairs):
        stats = mix(h, top, weights, stats)
    first = stats.astype(jnp.bfloat16).astype(jnp.float32)
    left = stats - first
    second = left.astype(jnp.bfloat16).astype(jnp.float32)
    is_second = (part == 1) | (part == TOPS + 1)
    stats = jnp.where(is_second, second, jnp.where(part == 2, left - second, first))
    stats = stats.astype(jnp.bfloat16)
    for i, ref in enumerate(o_refs):
        ref[:, width:] = stats[i * rows : (i + 1) * rows]


def own_halves(width):
    own = lax.rem(lax.axis_index("team"), 2)
    return [pl.ds(pl.multiple_of(half * width, HD), width) for half in (own, 1 - own)]


def split_keys_kernel(n_whole, *refs):
    whole_refs, out_refs = refs[:n_whole], refs[n_whole:]
    rows, halves = whole_refs[0].shape[0], own_halves(out_refs[0].shape[1])
    for m, out_ref in enumerate(out_refs):
        for i, whole_ref in enumerate(whole_refs):
            out_ref[i * rows : (i + 1) * rows] = whole_ref[:, halves[m % 2]]


def join_queries_kernel(own_ref, whole_ref, out_ref):
    rows, width = own_ref.shape
    out_ref[:rows] = own_ref[...]
    out_ref[rows:] = whole_ref[:, own_halves(width)[0]]


def merge_kernel(*refs):
    pieces, out_ref = refs[:-1], refs[-1]
    width = pieces[0].shape[1] - HD
    tops, totals = [], []
    for ref in pieces:
        stats = ref[:, width:].astype(jnp.float32)
        shifted = [stats] + [pltpu.roll(stats, HD - i * GAP, 1) for i in range(1, PARTS)]
        tops.append(shifted[0] + shifted[1] + shifted[2])
        totals.append(shifted[3] + shifted[4])
    common = tops[0]
    for top in tops[1:]:
        common = jnp.maximum(common, top)
    factors = [jnp.exp2(top - common) for top in tops]
    row_sum = sum(f * t for f, t in zip(factors, totals))
    factors = [f / row_sum for f in factors]
    for h in range(width // HD):
        columns = slice(h * HD, (h + 1) * HD)
        mixed = sum(
            f[:, h : h + 1] * ref[:, columns].astype(jnp.float32) for f, ref in zip(factors, pieces)
        )
        out_ref[:, columns] = mixed.astype(out_ref.dtype)


def finish_kernel(other_ref, own_ref, answer_ref, out_ref, own_half, sems):
    width = other_ref.shape[1]
    half = lax.rem(lax.axis_index("team"), 2)
    copies = [
        pltpu.make_async_copy(
            source, out_ref.at[:, pl.ds(pl.multiple_of(which * width, HD), width)], sems.at[i]
        )
        for i, (source, which) in enumerate(((other_ref, 1 - half), (own_half, half)))
    ]
    copies[0].start()
    merge_kernel(own_ref, answer_ref, own_half)
    copies[1].start()
    for copy in copies:
        copy.wait()


def paired(queries, key_rows, value_rows):
    rows = queries.shape[0]
    width = queries.shape[1] // 2
    planes, members = lax.axis_size("blk"), lax.axis_size("team")

    def shape(n_rows, columns):
        return jax.ShapeDtypeStruct((n_rows, columns), queries.dtype)

    def send(array, plane_bits, member_bits):
        pairs = [
            (z * members + m, (z ^ plane_bits) * members + (m ^ member_bits))
            for z in range(planes)
            for m in range(members)
        ]
        return lax.ppermute(array, ("blk", "team"), pairs)

    def small(kernel, shapes, *arrays):
        return pl.pallas_call(
            kernel,
            out_shape=shapes,
            in_specs=[vmem_spec()] * len(arrays),
            out_specs=[vmem_spec()] * len(shapes),
            compiler_params=params(),
        )(*arrays)

    far = range(2, planes, 2)
    whole = [send(key_rows, p, 0) for p in far]
    asked = send(queries, 0, 1)
    kv_own, kv_other, v_own, v_other, q_own = pack(
        (
            ((0, 0), (1, 0)),
            ((0, 1), (1, 1)),
            ((1, 0),),
            ((1, 1),),
            ((2, 0),),
        ),
        key_rows,
        value_rows,
        queries,
    )
    beside = [kv_own, send(kv_other, 0, 1)]
    beside += [send(kv_other if m % 2 else kv_own, 0, m) for m in range(2, members)]
    k_parts, v_parts = [(piece, 0) for piece in beside], [(piece, rows) for piece in beside]
    v_parts += [(send(v_other if m % 2 else v_own, p, m), 0) for p in far for m in range(members)]
    (joined,) = small(join_queries_kernel, [shape(2 * rows, width)], q_own, asked)
    both = send(joined, 1, 0)
    q_parts = [(joined, 0), (joined, rows), (both, 0), (both, rows)]
    mine, *theirs = small(
        partial(split_keys_kernel, len(whole)), [shape(len(far) * rows, width)] * members, *whole
    )
    shared = [mine] + [send(theirs[m - 1], 0, m) for m in range(1, members)]
    k_parts += [(piece, i * rows) for piece in shared for i in range(len(far))]
    operands = list({id(piece): piece for piece, _ in k_parts + v_parts + q_parts}.values())
    place = {id(piece): i for i, piece in enumerate(operands)}
    k_at, v_at, q_at = (
        [(place[id(piece)], row) for piece, row in parts] for parts in (k_parts, v_parts, q_parts)
    )
    own, *answers = pl.pallas_call(
        partial(attend_kernel, rows, k_at, v_at, q_at),
        out_shape=[shape(rows, width + HD)] * len(q_at),
        in_specs=[vmem_spec()] * len(operands),
        out_specs=[vmem_spec()] * len(q_at),
        compiler_params=params(),
        name="attend",
    )(*operands)
    back_near = send(answers[0], 0, 1)
    back_ask = send(answers[1], 1, 0)
    back_cross = send(answers[2], 1, 1)
    early = pl.pallas_call(
        merge_kernel,
        out_shape=shape(rows, width),
        in_specs=[vmem_spec()] * 2,
        out_specs=vmem_spec(),
        compiler_params=params(),
        name="merge",
    )(back_near, back_cross)
    return pl.pallas_call(
        finish_kernel,
        out_shape=shape(rows, 2 * width),
        in_specs=[vmem_spec()] * 3,
        out_specs=pl.BlockSpec(memory_space=pl.ANY),
        scratch_shapes=[pltpu.VMEM((rows, width), queries.dtype), pltpu.SemaphoreType.DMA((2,))],
        compiler_params=params(),
        name="finish",
    )(early, own, back_ask)


def solution(mesh):
    spec = P(("groups", "blk", "team"), "head")
    planes, members = mesh.shape["blk"], mesh.shape["team"]
    in_quads = planes > 2 and members > 1 and all(n & (n - 1) == 0 for n in (planes, members))

    def local(queries, key_rows, value_rows):
        heads = queries.shape[1] // HD
        plan = paired if in_quads and heads % 2 == 0 and heads // 2 <= GAP else gathered
        return plan(queries, key_rows, value_rows)

    return jax.shard_map(local, mesh=mesh, in_specs=(spec,) * 3, out_specs=spec, check_vma=False)
```

```python
from functools import partial
import math

import jax
import jax.numpy as jnp
from jax import lax
from jax.experimental import pallas as pl
from jax.experimental.pallas import tpu as pltpu
from jax.sharding import PartitionSpec as P


HD = 128
T_DEV = 48


def attend_block(running, key_block, value_block, query_rows, score_scale):
    row_top, row_total, weighted = running
    scores = (
        jnp.einsum("qhd,khd->qhk", query_rows, key_block, preferred_element_type=jnp.float32)
        * score_scale
    )
    new_top = jnp.maximum(row_top, jnp.max(scores, axis=2))
    shrink = jnp.exp(row_top - new_top)
    weights = jnp.exp(scores - new_top[:, :, None])
    row_total = row_total * shrink + jnp.sum(weights, axis=2)
    weighted = weighted * shrink[:, :, None] + jnp.einsum(
        "qhk,khd->qhd",
        weights.astype(jnp.bfloat16),
        value_block,
        preferred_element_type=jnp.float32,
    )
    return (new_top, row_total, weighted)


def fold_piece(running, shard_piece, query_rows, score_scale):
    key_piece, value_piece = shard_piece
    piece_rows = key_piece.shape[0]
    block_rows = T_DEV
    local_heads = query_rows.shape[1]
    key_blocks = key_piece.reshape(piece_rows // block_rows, block_rows, local_heads, HD)
    value_blocks = value_piece.reshape(piece_rows // block_rows, block_rows, local_heads, HD)

    def one_block(current, block_pair):
        return (attend_block(current, block_pair[0], block_pair[1], query_rows, score_scale), None)

    running, _ = lax.scan(one_block, running, (key_blocks, value_blocks))
    return running


def gathered(queries, key_rows, value_rows):
    own_rows = queries.shape[0]
    local_heads = queries.shape[1] // HD
    score_scale = 1.0 / math.sqrt(HD)
    team_queries = lax.all_gather(queries, "team", axis=0, tiled=True)
    team_count = team_queries.shape[0]
    query_heads = team_queries.reshape(team_count, local_heads, HD)
    folder = partial(fold_piece, query_rows=query_heads, score_scale=score_scale)
    row_top, row_total, weighted = folder(
        (
            jnp.full((team_count, local_heads), -1e30, jnp.float32),
            jnp.zeros((team_count, local_heads), jnp.float32),
            jnp.zeros((team_count, local_heads, HD), jnp.float32),
        ),
        (
            lax.all_gather(key_rows, "blk", axis=0, tiled=True),
            lax.all_gather(value_rows, "blk", axis=0, tiled=True),
        ),
    )
    swapped, member_tops, totals = (
        lax.all_to_all(
            weighted.reshape(team_count, local_heads * HD),
            "team",
            split_axis=0,
            concat_axis=0,
            tiled=True,
        ),
        lax.all_to_all(row_top, "team", split_axis=0, concat_axis=0, tiled=True),
        lax.all_to_all(row_total, "team", split_axis=0, concat_axis=0, tiled=True),
    )
    members = lax.axis_size("team")
    member_tops = member_tops.reshape(members, own_rows, local_heads)
    common_top = jnp.max(member_tops, axis=0)
    factor = jnp.exp(member_tops - common_top[None])
    row_sum = jnp.sum(factor * totals.reshape(members, own_rows, local_heads), axis=0)
    summed = jnp.sum(
        factor[:, :, :, None] * swapped.reshape(members, own_rows, local_heads, HD), axis=0
    )
    mixed_rows = summed / row_sum[:, :, None]
    return mixed_rows.reshape(own_rows, local_heads * HD).astype(jnp.bfloat16)


TOPS, PARTS = 3, 5
GAP = 128 // 8


def vmem_spec():
    return pl.BlockSpec(memory_space=pltpu.VMEM)


def hbm_array(array):
    return pltpu.with_memory_space_constraint(array, pltpu.HBM)


def params():
    return pltpu.CompilerParams(vmem_limit_bytes=16 * 2**20)


def pack_kernel(width, pieces, *refs):
    n_outs = len(pieces)
    sems = refs[-1]
    args, outs = refs[: -1 - n_outs], refs[-1 - n_outs : -1]
    rows = args[0].shape[0]
    own = lax.rem(lax.axis_index("team"), 2)
    halves = [pl.ds(pl.multiple_of(h * width, HD), width) for h in (own, 1 - own)]
    copies = []
    for parts, out in zip(pieces, outs):
        for i, (arg, half) in enumerate(parts):
            source = args[arg].at[:, halves[half]]
            target = out.at[pl.ds(i * rows, rows)]
            copies.append(pltpu.make_async_copy(source, target, sems.at[len(copies)]))
            copies[-1].start()
    for copy in copies:
        copy.wait()


def pack(pieces, *arrays):
    rows, width = arrays[0].shape[0], arrays[0].shape[1] // 2
    return pl.pallas_call(
        partial(pack_kernel, width, pieces),
        out_shape=[
            jax.ShapeDtypeStruct((len(parts) * rows, width), arrays[0].dtype) for parts in pieces
        ],
        in_specs=[pl.BlockSpec(memory_space=pltpu.HBM)] * len(arrays),
        out_specs=[vmem_spec()] * len(pieces),
        scratch_shapes=[pltpu.SemaphoreType.DMA((sum(map(len, pieces)),))],
        compiler_params=params(),
        name="pack",
    )(*map(hbm_array, arrays))


def attend_kernel(rows, k_at, v_at, q_at, *refs):
    o_refs = refs[-len(q_at) :]
    width = o_refs[0].shape[1] - HD
    scale = math.log2(math.e) / math.sqrt(HD)
    lane = lax.broadcasted_iota(jnp.int32, (len(q_at) * rows, HD), 1)
    slot, part = lax.rem(lane, GAP), lax.div(lane, GAP)
    stats = jnp.zeros(lane.shape, jnp.float32)

    def load(places, h):
        columns = slice(h * HD, (h + 1) * HD)
        return jnp.concatenate([refs[i][row : row + rows, columns] for i, row in places], axis=0)

    def score(h):
        q, k = load(q_at, h), load(k_at, h)
        product = lax.dot_general(
            q, k, (((1,), (1,)), ((), ())), preferred_element_type=jnp.float32
        )
        return product

    def weigh(scores):
        top = jnp.max(scores, axis=1, keepdims=True)
        return top * scale, jnp.exp2((scores - top) * scale).astype(jnp.bfloat16)

    def mix(h, top, weights, stats):
        v = load(v_at, h)
        v = jnp.concatenate([v, jnp.ones_like(v)], axis=1)
        mixed = jnp.dot(weights, v, preferred_element_type=jnp.float32)
        for i, ref in enumerate(o_refs):
            ref[:, h * HD : (h + 1) * HD] = mixed[i * rows : (i + 1) * rows, :HD].astype(ref.dtype)
        return jnp.where(slot == h, jnp.where(part < TOPS, top, mixed[:, HD:]), stats)

    heads = width // HD
    scores = [score(h) for h in range(heads)]
    pairs = [weigh(s) for s in scores]
    for h, (top, weights) in enumerate(pairs):
        stats = mix(h, top, weights, stats)
    first = stats.astype(jnp.bfloat16).astype(jnp.float32)
    left = stats - first
    second = left.astype(jnp.bfloat16).astype(jnp.float32)
    is_second = (part == 1) | (part == TOPS + 1)
    stats = jnp.where(is_second, second, jnp.where(part == 2, left - second, first))
    stats = stats.astype(jnp.bfloat16)
    for i, ref in enumerate(o_refs):
        ref[:, width:] = stats[i * rows : (i + 1) * rows]


def own_halves(width):
    own = lax.rem(lax.axis_index("team"), 2)
    return [pl.ds(pl.multiple_of(half * width, HD), width) for half in (own, 1 - own)]


def split_keys_kernel(n_whole, *refs):
    whole_refs, out_refs = refs[:n_whole], refs[n_whole:]
    rows, halves = whole_refs[0].shape[0], own_halves(out_refs[0].shape[1])
    for m, out_ref in enumerate(out_refs):
        for i, whole_ref in enumerate(whole_refs):
            out_ref[i * rows : (i + 1) * rows] = whole_ref[:, halves[m % 2]]


def join_queries_kernel(own_ref, whole_ref, out_ref):
    rows, width = own_ref.shape
    out_ref[:rows] = own_ref[...]
    out_ref[rows:] = whole_ref[:, own_halves(width)[0]]


def merge_kernel(*refs):
    pieces, out_ref = refs[:-1], refs[-1]
    width = pieces[0].shape[1] - HD
    tops, totals = [], []
    for ref in pieces:
        stats = ref[:, width:].astype(jnp.float32)
        shifted = [stats] + [pltpu.roll(stats, HD - i * GAP, 1) for i in range(1, PARTS)]
        tops.append(shifted[0] + shifted[1] + shifted[2])
        totals.append(shifted[3] + shifted[4])
    common = tops[0]
    for top in tops[1:]:
        common = jnp.maximum(common, top)
    factors = [jnp.exp2(top - common) for top in tops]
    row_sum = sum(f * t for f, t in zip(factors, totals))
    factors = [f / row_sum for f in factors]
    for h in range(width // HD):
        columns = slice(h * HD, (h + 1) * HD)
        mixed = sum(
            f[:, h : h + 1] * ref[:, columns].astype(jnp.float32) for f, ref in zip(factors, pieces)
        )
        out_ref[:, columns] = mixed.astype(out_ref.dtype)


def finish_kernel(other_ref, own_ref, answer_ref, out_ref, own_half, sems):
    width = other_ref.shape[1]
    half = lax.rem(lax.axis_index("team"), 2)
    copies = [
        pltpu.make_async_copy(
            source, out_ref.at[:, pl.ds(pl.multiple_of(which * width, HD), width)], sems.at[i]
        )
        for i, (source, which) in enumerate(((other_ref, 1 - half), (own_half, half)))
    ]
    copies[0].start()
    merge_kernel(own_ref, answer_ref, own_half)
    copies[1].start()
    for copy in copies:
        copy.wait()


def paired(queries, key_rows, value_rows):
    rows = queries.shape[0]
    width = queries.shape[1] // 2
    planes, members = lax.axis_size("blk"), lax.axis_size("team")

    def shape(n_rows, columns):
        return jax.ShapeDtypeStruct((n_rows, columns), queries.dtype)

    def send(array, plane_bits, member_bits):
        pairs = [
            (z * members + m, (z ^ plane_bits) * members + (m ^ member_bits))
            for z in range(planes)
            for m in range(members)
        ]
        return lax.ppermute(array, ("blk", "team"), pairs)

    def small(kernel, shapes, *arrays):
        return pl.pallas_call(
            kernel,
            out_shape=shapes,
            in_specs=[vmem_spec()] * len(arrays),
            out_specs=[vmem_spec()] * len(shapes),
            compiler_params=params(),
        )(*arrays)

    far = range(2, planes, 2)
    whole = [send(key_rows, p, 0) for p in far]
    asked = send(queries, 0, 1)
    kv_own, kv_other, v_own, v_other, q_own = pack(
        (
            ((0, 0),) if members == 2 else ((0, 0), (1, 0)),
            ((0, 1), (1, 1)),
            ((1, 0),),
            ((1, 1),),
            ((2, 0),),
        ),
        key_rows,
        value_rows,
        queries,
    )
    beside = [kv_own, send(kv_other, 0, 1)]
    beside += [send(kv_other if m % 2 else kv_own, 0, m) for m in range(2, members)]
    k_parts, v_parts = [(piece, 0) for piece in beside], [(piece, rows) for piece in beside]
    v_parts[0] = (v_own, 0)
    v_parts += [(send(v_other if m % 2 else v_own, p, m), 0) for p in far for m in range(members)]
    (joined,) = small(join_queries_kernel, [shape(2 * rows, width)], q_own, asked)
    both = send(joined, 1, 0)
    q_parts = [(joined, 0), (joined, rows), (both, 0), (both, rows)]
    mine, *theirs = small(
        partial(split_keys_kernel, len(whole)), [shape(len(far) * rows, width)] * members, *whole
    )
    shared = [mine] + [send(theirs[m - 1], 0, m) for m in range(1, members)]
    k_parts += [(piece, i * rows) for piece in shared for i in range(len(far))]
    operands = list({id(piece): piece for piece, _ in k_parts + v_parts + q_parts}.values())
    place = {id(piece): i for i, piece in enumerate(operands)}
    k_at, v_at, q_at = (
        [(place[id(piece)], row) for piece, row in parts] for parts in (k_parts, v_parts, q_parts)
    )
    own, *answers = pl.pallas_call(
        partial(attend_kernel, rows, k_at, v_at, q_at),
        out_shape=[shape(rows, width + HD)] * len(q_at),
        in_specs=[vmem_spec()] * len(operands),
        out_specs=[vmem_spec()] * len(q_at),
        compiler_params=params(),
        name="attend",
    )(*operands)
    back_near = send(answers[0], 0, 1)
    back_ask = send(answers[1], 1, 0)
    back_cross = send(answers[2], 1, 1)
    early = pl.pallas_call(
        merge_kernel,
        out_shape=shape(rows, width),
        in_specs=[vmem_spec()] * 2,
        out_specs=vmem_spec(),
        compiler_params=params(),
        name="merge",
    )(back_near, back_cross)
    return pl.pallas_call(
        finish_kernel,
        out_shape=shape(rows, 2 * width),
        in_specs=[vmem_spec()] * 3,
        out_specs=pl.BlockSpec(memory_space=pl.ANY),
        scratch_shapes=[pltpu.VMEM((rows, width), queries.dtype), pltpu.SemaphoreType.DMA((2,))],
        compiler_params=params(),
        name="finish",
    )(early, own, back_ask)


def solution(mesh):
    spec = P(("groups", "blk", "team"), "head")
    planes, members = mesh.shape["blk"], mesh.shape["team"]
    in_quads = planes > 2 and members > 1 and all(n & (n - 1) == 0 for n in (planes, members))

    def local(queries, key_rows, value_rows):
        heads = queries.shape[1] // HD
        plan = paired if in_quads and heads % 2 == 0 and heads // 2 <= GAP else gathered
        return plan(queries, key_rows, value_rows)

    return jax.shard_map(local, mesh=mesh, in_specs=(spec,) * 3, out_specs=spec, check_vma=False)
```
